32 devices in a mesh: groups: 2 (over x), graph: 16 (over z, y, core).
Axes of the slice: x: 2, y: 2, z: 4, core: 2. Of those that a mesh axis runs over, the one named last changes fastest.
Arguments:
- edge_state: bfloat16 [32768, 512], P(('groups', 'graph')), parts along dimension 0, may hold values from -6 to 6
- atom_state: bfloat16 [4096, 256], P(('groups', 'graph')), parts along dimension 0, may hold values from -6 to 6
- block_atom: int32 [1024], P(('groups', 'graph')), parts along dimension 0, may hold values from 0 to 127, as said below
- target_row: int32 [32768], P(('groups', 'graph')), parts along dimension 0, may hold values from 0 to 15
- reverse_block: int32 [1024], P(('groups', 'graph')), parts along dimension 0, may hold values from 0 to 511, as said below
- reverse_lane: int32 [32768], P(('groups', 'graph')), parts along dimension 0, may hold values from 0 to 31, as said below
- source_atom: int32 [32768], P(('groups', 'graph')), parts along dimension 0, may hold values from 0 to 127, as said below
- edge_weights: bfloat16 [2, 4, 512, 512], replicated, may hold values from -0.25 to 0.25
- atom_in_weights: bfloat16 [2, 2, 256, 512], replicated, may hold values from -0.375 to 0.375
- atom_out_weights: bfloat16 [2, 512, 256], replicated, may hold values from -0.25 to 0.25
Outputs:
- edge_out: bfloat16 [32768, 512], P(('groups', 'graph')), parts along dimension 0
- atom_out: bfloat16 [4096, 256], P(('groups', 'graph')), parts along dimension 0
The draws below stay inside these ranges and needn't reach their ends.
There are 2 independent parts, one for each index of `groups`. The reference program is written for one: setup_inputs(seed, part) draws one part's arguments, and reference() takes and returns one part's arrays. A program takes and returns all parts, laid end to end along the dimension named above; an argument that names none is the same for every part. Nothing has to cross between parts.
Inputs may be any that keep to these rules, and one draw needn't show every extreme that they name: `block_atom`: among the 32 edge blocks of one device, at most 4 name atom blocks held by any one device (device k holds atom blocks k * 8 to (k + 1) * 8 - 1), and for every device some one device is named exactly 4 times. `reverse_block`: an involution without fixed points. The partner of a block of device k lies on device k - 1, k or k + 1 (no wrap); every device but the last has exactly 8 blocks paired with the device above, every device but the first exactly 8 paired with the device below. `reverse_lane`: together with reverse_block, the map from an edge to its reverse edge is an involution. `source_atom`: Non-decreasing over the edges of one device, and every one of the device's 128 atoms is the source of at least one of its edges.
All inputs are finite; a program needn't handle non-finite values.
Results may differ from the reference program's by a relative error of at most 0.019.
Values may be sent and summed in bfloat16 or wider, within the bound.
A program may use at most 64 MiB of HBM per device.

```python
import jax
import jax.numpy as jnp

DE = 512
DA = 256
NB = 32
ATB = 16
CAP = 4
LAYERS = 2
E_DEV = 1024
EBLK_DEV = 32
A_DEV = 128
ABLK_DEV = 8
EDGES = 16384
ATOMS = 2048
EBLOCKS = 512


def draw_block_atom(key, part):
    peer_total = EBLOCKS // EBLK_DEV

    def one_device(device_key):
        busiest = jax.random.randint(jax.random.fold_in(device_key, 1), (), 0, peer_total).astype(jnp.int32)
        slot_ids = jnp.arange(peer_total * CAP, dtype=jnp.int32)
        slot_owner = slot_ids // CAP
        scores = jax.random.randint(jax.random.fold_in(device_key, 2), (peer_total * CAP,), 0, 4096).astype(jnp.int32) * (peer_total * CAP) + slot_ids
        scores = jnp.where(slot_owner == busiest, 2 ** 30, scores)
        ranking = jnp.argsort(scores, stable=True)
        others = slot_owner[ranking[:EBLK_DEV - CAP]]
        owners = jnp.concatenate([jnp.full((CAP,), busiest, jnp.int32), others])
        shuffle_scores = jax.random.randint(jax.random.fold_in(device_key, 3), (EBLK_DEV,), 0, 4096).astype(jnp.int32) * EBLK_DEV + jnp.arange(EBLK_DEV, dtype=jnp.int32)
        owners = owners[jnp.argsort(shuffle_scores, stable=True)]
        local_block = jax.random.randint(jax.random.fold_in(device_key, 4), (EBLK_DEV,), 0, ABLK_DEV).astype(jnp.int32)
        return owners * ABLK_DEV + local_block
    device_keys = jax.random.split(jax.random.fold_in(key, 5), peer_total)
    return jax.vmap(one_device)(device_keys).reshape(-1).astype(jnp.int32)


def reverse_pairs(key):
    peer_total = EBLOCKS // EBLK_DEV
    quarter = EBLK_DEV // 4
    base_key = jax.random.fold_in(key, 11)
    scores = jax.random.randint(jax.random.fold_in(base_key, 1), (peer_total, EBLK_DEV), 0, 4096).astype(jnp.int32) * EBLK_DEV + jnp.arange(EBLK_DEV, dtype=jnp.int32)[None, :]
    arrange = jnp.argsort(scores, axis=1, stable=True).astype(jnp.int32)
    device_grid = jnp.arange(peer_total, dtype=jnp.int32)[:, None] + jnp.zeros((1, EBLK_DEV), jnp.int32)
    position = jnp.arange(EBLK_DEV, dtype=jnp.int32)[None, :] + jnp.zeros((peer_total, 1), jnp.int32)
    upper_group = position < quarter
    lower_group = (position >= quarter) & (position < 2 * quarter)
    inner_position = 2 * quarter + jnp.bitwise_xor(position - 2 * quarter, 1)
    has_upper = device_grid < peer_total - 1
    has_lower = device_grid > 0
    partner_device = jnp.where(upper_group & has_upper, device_grid + 1, jnp.where(lower_group & has_lower, device_grid - 1, device_grid))
    partner_position = jnp.where(upper_group, jnp.where(has_upper, position + quarter, jnp.bitwise_xor(position, 1)), jnp.where(lower_group, jnp.where(has_lower, position - quarter, quarter + jnp.bitwise_xor(position - quarter, 1)), inner_position))
    own_block = device_grid * EBLK_DEV + arrange
    partner_block = partner_device * EBLK_DEV + arrange[partner_device, partner_position]
    reverse = jnp.zeros((EBLOCKS,), jnp.int32).at[own_block.reshape(-1)].set(partner_block.reshape(-1))
    block_ids = jnp.arange(EBLOCKS, dtype=jnp.int32)
    lower_end = jnp.minimum(block_ids, reverse)
    lane_key = jax.random.fold_in(key, 12)

    def lane_order(block_number):
        lane_scores = jax.random.randint(jax.random.fold_in(lane_key, block_number), (NB,), 0, 4096).astype(jnp.int32) * NB + jnp.arange(NB, dtype=jnp.int32)
        return jnp.argsort(lane_scores, stable=True).astype(jnp.int32)
    forward = jax.vmap(lane_order)(lower_end)
    backward = jnp.argsort(forward, axis=1, stable=True).astype(jnp.int32)
    lanes = jnp.where((block_ids < reverse)[:, None], forward, backward)
    return (reverse, lanes.reshape(-1).astype(jnp.int32))


def draw_reverse_block(key, part):
    return reverse_pairs(key)[0]


def draw_reverse_lane(key, part):
    return reverse_pairs(key)[1]


def draw_source_atom(key, part):
    peer_total = EDGES // E_DEV

    def one_device(device_key):
        places = jnp.arange(1, E_DEV, dtype=jnp.int32)
        scores = jax.random.randint(device_key, (E_DEV - 1,), 0, 4096).astype(jnp.int32) * E_DEV + places
        cut_points = places[jnp.argsort(scores, stable=True)[:A_DEV - 1]]
        edge_ids = jnp.arange(E_DEV, dtype=jnp.int32)
        return jnp.sum((cut_points[None, :] <= edge_ids[:, None]).astype(jnp.int32), axis=1)
    device_keys = jax.random.split(jax.random.fold_in(key, 21), peer_total)
    return jax.vmap(one_device)(device_keys).reshape(-1).astype(jnp.int32)


def place_ends(entries, rng, smallest, high):
    extent = entries.shape
    place = [jax.random.randint(jax.random.fold_in(rng, axis), (), 0, extent[axis]) for axis in range(len(extent))]
    entries = entries.at[tuple(place)].set(smallest)
    longest = extent.index(max(extent))
    place[longest] = (place[longest] + 1) % extent[longest]
    return entries.at[tuple(place)].set(high)


def block_scale(rng, extent, cuts, smallest, high):
    factor_of = 1.0
    for axis_at, blocks in cuts:
        heights = jax.random.uniform(jax.random.fold_in(jax.random.fold_in(rng, 6), axis_at), (blocks,), jnp.float32, smallest / len(cuts), high / len(cuts))
        factor_of = factor_of * jnp.repeat(jnp.exp(heights), extent[axis_at] // blocks).reshape((-1,) + (1,) * (len(extent) - 1 - axis_at))
    return factor_of


def scatter_about(own_key, shape, scale, reach, shards=(), kind=jnp.bfloat16):
    gain = block_scale(own_key, shape, shards, -0.22, 0.18) if shards else 1.0
    drawn = jax.random.normal(own_key, shape, jnp.float32) * scale * gain
    return jnp.minimum(jnp.maximum(drawn, -reach), reach).astype(kind)


def setup_inputs(seed: int = 0, part: int = 0) -> dict:
    key_list = jax.random.split(jax.random.key(seed), 11)
    own_keys = jax.random.split(jax.random.fold_in(key_list[10], part), 11)
    edge_state = scatter_about(own_keys[0], (EDGES, DE), 1.0, 6.0, ((0, 16),))
    atom_state = scatter_about(own_keys[1], (ATOMS, DA), 1.0, 6.0, ((0, 16),))
    block_atom = draw_block_atom(jax.random.fold_in(jax.random.fold_in(key_list[10], part), 71), part)
    target_row = place_ends(jax.random.randint(own_keys[3], (EDGES,), 0, ATB), jax.random.fold_in(own_keys[3], 1), 0, ATB - 1).astype(jnp.int32)
    reverse_block = draw_reverse_block(jax.random.fold_in(jax.random.fold_in(key_list[10], part), 71), part)
    reverse_lane = draw_reverse_lane(jax.random.fold_in(jax.random.fold_in(key_list[10], part), 71), part)
    source_atom = draw_source_atom(jax.random.fold_in(jax.random.fold_in(key_list[10], part), 71), part)
    edge_weights = scatter_about(key_list[7], (LAYERS, 4, DE, DE), DE ** -0.5, 0.25)
    atom_in_weights = scatter_about(key_list[8], (LAYERS, 2, DA, DE), DA ** -0.5, 0.375)
    atom_out_weights = scatter_about(key_list[9], (LAYERS, DE, DA), DE ** -0.5, 0.25)
    return dict(edge_state=edge_state, atom_state=atom_state, block_atom=block_atom, target_row=target_row, reverse_block=reverse_block, reverse_lane=reverse_lane, source_atom=source_atom, edge_weights=edge_weights, atom_in_weights=atom_in_weights, atom_out_weights=atom_out_weights)


def reference(edge_state, atom_state, block_atom, target_row, reverse_block, reverse_lane, source_atom, edge_weights, atom_in_weights, atom_out_weights):
    target_index = jnp.repeat(block_atom, NB) * ATB + target_row
    edge_owner = jnp.arange(EDGES, dtype=jnp.int32) // E_DEV
    source_index = edge_owner * A_DEV + source_atom
    reverse_index = jnp.repeat(reverse_block, NB) * NB + reverse_lane
    edges_now = edge_state
    atoms_now = atom_state
    for layer_index in range(LAYERS):
        mixed = jnp.dot(edges_now, edge_weights[layer_index, 0], preferred_element_type=jnp.float32)
        mixed = mixed + jnp.dot(atoms_now[target_index], atom_in_weights[layer_index, 0], preferred_element_type=jnp.float32)
        mixed = mixed + jnp.dot(atoms_now[source_index], atom_in_weights[layer_index, 1], preferred_element_type=jnp.float32)
        hidden = jax.nn.silu(mixed).astype(jnp.bfloat16)
        updated = (edges_now.astype(jnp.float32) + jnp.dot(hidden, edge_weights[layer_index, 1], preferred_element_type=jnp.float32)).astype(jnp.bfloat16)
        paired = (updated.astype(jnp.float32) + updated[reverse_index].astype(jnp.float32)).astype(jnp.bfloat16)
        gated = jax.nn.silu(jnp.dot(paired, edge_weights[layer_index, 2], preferred_element_type=jnp.float32)).astype(jnp.bfloat16)
        edges_now = (updated.astype(jnp.float32) + jnp.dot(gated, edge_weights[layer_index, 3], preferred_element_type=jnp.float32)).astype(jnp.bfloat16)
        summed = jax.ops.segment_sum(edges_now.astype(jnp.float32), source_index, num_segments=ATOMS)
        pooled = (0.35 * summed).astype(jnp.bfloat16)
        atoms_now = (atoms_now.astype(jnp.float32) + jax.nn.silu(jnp.dot(pooled, atom_out_weights[layer_index], preferred_element_type=jnp.float32))).astype(jnp.bfloat16)
    return edges_now, atoms_now
```

```python
import functools

import jax
import jax.numpy as jnp
from jax import lax
from jax.experimental import pallas as pl
from jax.experimental.pallas import tpu as pltpu
from jax.sharding import PartitionSpec as P

NB = 32
ATB = 16
LAYERS = 2
EBLK = 32
A_DEV = 128
QUARTER = 8
CH = QUARTER * NB
MESH = pl.DeviceIdType.MESH
F32 = jnp.float32
BF16 = jnp.bfloat16


def dot(a, b):
    return jnp.dot(a, b, preferred_element_type=F32)


def silu(v):
    return (0.5 * v) * (1.0 + jnp.tanh(0.5 * v))


def hot(mask):
    return jnp.where(mask, 1.0, 0.0).astype(BF16)


def kernel(
    n,
    rblock,
    batom,
    edge_hbm,
    atom_in,
    trow,
    rlane,
    satom,
    ew_hbm,
    aw_hbm,
    ow_hbm,
    edge_out,
    atom_out,
    pos_out,
    raw,
    ohe,
    edges,
    upd,
    part,
    oht,
    ohs,
    ohr,
    ohc,
    table,
    recv_up,
    recv_dn,
    ew,
    aw,
    ow,
    load_sem,
    out_sem,
    ag_send,
    ag_recv,
    x_send,
    x_recv,
):
    me = lax.axis_index("graph")
    planes = n // 4
    y = (me // 2) % 2
    c = me % 2
    y_peer = me + 2 - 4 * y
    s_peer = me + 1 - 2 * c
    s_y_peer = s_peer + 2 - 4 * y
    has_up = me < n - 1
    has_dn = me > 0

    loads = [pltpu.make_async_copy(edge_hbm, raw, load_sem.at[0])]
    order = [(aw_hbm, aw, 0), (ew_hbm, ew, 0), (ow_hbm, ow, 0), (aw_hbm, aw, 1), (ew_hbm, ew, 1), (ow_hbm, ow, 1)]
    for i, (src, dst, l) in enumerate(order):
        loads.append(pltpu.make_async_copy(src.at[l], dst.at[l], load_sem.at[i + 1]))
    for cp in loads:
        cp.start()

    barrier = pltpu.get_barrier_semaphore()

    def greet(dev):
        pl.semaphore_signal(barrier, inc=1, device_id={"graph": dev}, device_id_type=MESH)

    for d in range(1, planes):
        greet((me + 4 * d) % n)
    greet(y_peer)
    greet(s_peer)

    greet((me + n + 2 * c - 1) % n)
    pl.semaphore_wait(barrier, planes + 2)

    def shard_rows(dev):
        return pl.ds(pl.multiple_of(dev * A_DEV, A_DEV), A_DEV)

    sent = []

    def push(l, shard, dev):
        rows = shard_rows(shard)
        cp = pltpu.make_async_remote_copy(
            src_ref=table.at[l, rows],
            dst_ref=table.at[l, rows],
            send_sem=ag_send.at[l, len(sent) % (4 * planes)],
            recv_sem=ag_recv.at[l, shard],
            device_id={"graph": dev},
            device_id_type=MESH,
        )
        cp.start()
        sent.append(cp)

    def arrived(l, shard):
        rows = shard_rows(shard)
        pltpu.make_async_remote_copy(
            src_ref=table.at[l, rows],
            dst_ref=table.at[l, rows],
            send_sem=ag_send.at[l, 0],
            recv_sem=ag_recv.at[l, shard],
            device_id={"graph": s_peer},
            device_id_type=MESH,
        ).wait_recv()

    def exchange(l, up):
        return pltpu.make_async_remote_copy(
            src_ref=upd.at[pl.ds(0 if up else CH, CH)],
            dst_ref=recv_dn.at[l] if up else recv_up.at[l],
            send_sem=x_send.at[l, 0 if up else 1],
            recv_sem=x_recv.at[l, 0 if up else 1],
            device_id={"graph": me + 1 if up else me - 1},
            device_id_type=MESH,
        )

    def block_order(key, is_up, is_dn, rank):
        n_up = jnp.where(has_up, QUARTER, 0)
        inner = rank - n_up - jnp.where(has_dn, QUARTER, 0)
        first_base = jnp.where(has_dn, jnp.where(has_up, 2 * QUARTER, 0), QUARTER)
        later_base = jnp.where(has_dn, jnp.where(has_up, 2 * QUARTER, QUARTER), QUARTER)
        inner = jnp.where(inner < QUARTER, inner + first_base, inner + later_base)
        return jnp.where(is_up, rank, jnp.where(is_dn, QUARTER + rank - n_up, inner))

    def prepare():
        square = (EBLK, EBLK)
        lanes = lax.broadcasted_iota(jnp.int32, square, 1)
        subs = lax.broadcasted_iota(jnp.int32, square, 0)
        rb = jnp.broadcast_to(rblock[...], square)
        low = me * EBLK
        is_up = rb >= low + EBLK
        is_dn = rb < low
        mine = lanes + low
        inner_key = 2 * jnp.minimum(mine, rb) + jnp.where(mine > rb, 1, 0)
        big = 4 * n * EBLK
        key = jnp.where(is_up, lanes, jnp.where(is_dn, big + rb, 2 * big + inner_key))
        rank = jnp.sum(jnp.where(key.T < key, 1, 0), axis=0, keepdims=True)
        pos = block_order(key, is_up, is_dn, jnp.broadcast_to(rank, square))
        pos_out[...] = pos[0:1, :]
        here = pos == subs
        pcol = jnp.sum(jnp.where(here, lanes, 0), axis=1, keepdims=True)
        bcol = jnp.sum(jnp.where(here, jnp.broadcast_to(batom[...], square), 0), axis=1, keepdims=True)
        pick = jnp.where(here, 1.0, 0.0).astype(BF16)

        def by_slot(ref):
            return dot(pick, ref[...].astype(F32).astype(BF16)).T.astype(jnp.int32)

        tcol = by_slot(trow)
        scol = by_slot(satom)
        rcol = by_slot(rlane)
        wide = lax.broadcasted_iota(jnp.int32, (NB, CH), 1)
        narrow = lax.broadcasted_iota(jnp.int32, (NB, A_DEV), 1)
        for p in range(EBLK):
            rows = pl.ds(p * NB, NB)
            oht[rows, :] = hot(wide == tcol[:, p : p + 1] + (p % 16) * ATB)
            ohs[rows, :] = hot(narrow == scol[:, p : p + 1])
            slot = p % QUARTER
            swapped = (slot ^ 1) * NB
            if p < 2 * QUARTER:
                remote = has_up if p < QUARTER else has_dn
                off = jnp.where(remote, slot * NB, swapped)
            else:
                off = swapped
            ohr[rows, :] = hot(wide == rcol[:, p : p + 1] + off)
        e_dev = raw.shape[0]
        from_edge = lax.broadcasted_iota(jnp.int32, (NB, e_dev), 1) - lax.broadcasted_iota(jnp.int32, (NB, e_dev), 0)
        for p in range(EBLK):
            ohe[pl.ds(p * NB, NB), :] = hot(from_edge == pcol[p : p + 1, :] * NB)
        atoms_all = n * A_DEV
        from_atom = lax.broadcasted_iota(jnp.int32, (ATB, atoms_all), 1) - lax.broadcasted_iota(jnp.int32, (ATB, atoms_all), 0)
        for p in range(EBLK):
            ohc[pl.ds(p * ATB, ATB), :] = hot(from_atom == bcol[p : p + 1, :] * ATB)

    def sort_edges():
        loads[0].wait()
        for q in range(4):
            rows = pl.ds(q * CH, CH)
            edges[rows, :] = dot(ohe[rows, :], raw[...]).astype(BF16)

    def result(q):
        rows = pl.ds(q * CH, CH)
        return pltpu.make_async_copy(edges.at[rows], edge_out.at[rows], out_sem.at[q])

    for l in range(LAYERS):
        atoms = atom_in if l == 0 else atom_out
        del sent[:]
        table[l, shard_rows(me), :] = atoms[...]
        for d in range(1, planes):
            push(l, me, (me + 4 * d) % n)
        push(l, me, y_peer)
        push(l, me, s_peer)

        if l == 0:
            prepare()
        for d in range(1, planes):
            shard = (me + n - 4 * d) % n
            arrived(l, shard)
            push(l, shard, y_peer)
            push(l, shard, s_peer)
        if l == 0:
            sort_edges()
            loads[1].wait()
            loads[2].wait()
        for d in range(planes):
            shard = (y_peer + n - 4 * d) % n
            arrived(l, shard)
            push(l, shard, s_peer)

        sproj = dot(atoms[...], aw[l, 1]).astype(BF16)
        for q in range(4):
            rows = pl.ds(q * CH, CH)
            part[rows, :] = dot(edges[rows, :], ew[l, 0]) + dot(ohs[rows, :], sproj)

        for d in range(planes):
            arrived(l, (s_peer + n - 4 * d) % n)
            arrived(l, (s_y_peer + n - 4 * d) % n)

        def project(half):
            chosen = dot(ohc[pl.ds(half * CH, CH), :], table[l]).astype(BF16)
            return dot(chosen, aw[l, 0]).astype(BF16)

        def first(q):
            rows = pl.ds(q * CH, CH)
            h = silu(part[rows, :] + dot(oht[rows, :], tproj)).astype(BF16)
            upd[rows, :] = (edges[rows, :].astype(F32) + dot(h, ew[l, 1])).astype(BF16)

        tproj = project(0)
        first(0)

        @pl.when(has_up)
        def _():
            exchange(l, True).start()

        first(1)

        @pl.when(has_dn)
        def _():
            exchange(l, False).start()

        tproj = project(1)
        first(2)
        first(3)

        if l == 0:
            loads[3].wait()

        def second(q, partner):
            rows = pl.ds(q * CH, CH)
            u = upd[rows, :].astype(F32)
            paired = (u + dot(ohr[rows, :], partner)).astype(BF16)
            g = silu(dot(paired, ew[l, 2])).astype(BF16)
            e = (u + dot(g, ew[l, 3])).astype(BF16)
            edges[rows, :] = e
            if l == LAYERS - 1:
                result(q).start()
            return lax.dot_general(ohs[rows, :], e, (((0,), (0,)), ((), ())), preferred_element_type=F32)

        summed = second(2, upd[pl.ds(2 * CH, CH), :])
        summed = summed + second(3, upd[pl.ds(3 * CH, CH), :])

        @pl.when(has_up)
        def _():
            exchange(l, False).wait_recv()

        @pl.when(jnp.logical_not(has_up))
        def _():
            recv_up[l] = upd[pl.ds(0, CH), :]

        summed = summed + second(0, recv_up[l])

        @pl.when(has_dn)
        def _():
            exchange(l, True).wait_recv()

        @pl.when(jnp.logical_not(has_dn))
        def _():
            recv_dn[l] = upd[pl.ds(CH, CH), :]

        summed = summed + second(1, recv_dn[l])

        pooled = (0.35 * summed).astype(BF16)
        atom_out[...] = (atoms[...].astype(F32) + silu(dot(pooled, ow[l]))).astype(BF16)

        for cp in sent:
            cp.wait_send()

        @pl.when(has_up)
        def _():
            exchange(l, True).wait_send()

        @pl.when(has_dn)
        def _():
            exchange(l, False).wait_send()

        if l == 0:
            for cp in loads[4:]:
                cp.wait()

    for q in range(4):
        result(q).wait()


def unsort(pos, src, dst, sem):
    for b in range(EBLK):
        start = pl.multiple_of(pos[0, b] * NB, NB)
        pltpu.make_async_copy(src.at[pl.ds(start, NB)], dst.at[pl.ds(b * NB, NB)], sem).start()
    pltpu.make_async_copy(src, dst, sem).wait()


def local(
    n,
    edge_state,
    atom_state,
    block_atom,
    target_row,
    reverse_block,
    reverse_lane,
    source_atom,
    edge_weights,
    atom_in_weights,
    atom_out_weights,
):
    de = edge_state.shape[1]
    da = atom_state.shape[1]
    e_dev = edge_state.shape[0]
    vmem = pl.BlockSpec(memory_space=pltpu.VMEM)
    smem = pl.BlockSpec(memory_space=pltpu.SMEM)
    anys = pl.BlockSpec(memory_space=pl.ANY)
    planes = n // 4
    ordered, atoms, pos = pl.pallas_call(
        functools.partial(kernel, n),
        out_shape=(
            jax.ShapeDtypeStruct((e_dev, de), BF16),
            jax.ShapeDtypeStruct((A_DEV, da), BF16),
            jax.ShapeDtypeStruct((1, EBLK), jnp.int32),
        ),
        in_specs=[vmem, vmem, anys, vmem, vmem, vmem, vmem, anys, anys, anys],
        out_specs=(anys, vmem, vmem),
        scratch_shapes=[
            pltpu.VMEM((e_dev, de), BF16),
            pltpu.VMEM((e_dev, e_dev), BF16),
            pltpu.VMEM((e_dev, de), BF16),
            pltpu.VMEM((e_dev, de), BF16),
            pltpu.VMEM((e_dev, de), F32),
            pltpu.VMEM((e_dev, CH), BF16),
            pltpu.VMEM((e_dev, A_DEV), BF16),
            pltpu.VMEM((e_dev, CH), BF16),
            pltpu.VMEM((EBLK * ATB, n * A_DEV), BF16),
            pltpu.VMEM((LAYERS, n * A_DEV, da), BF16),
            pltpu.VMEM((LAYERS, CH, de), BF16),
            pltpu.VMEM((LAYERS, CH, de), BF16),
            pltpu.VMEM(edge_weights.shape, BF16),
            pltpu.VMEM(atom_in_weights.shape, BF16),
            pltpu.VMEM(atom_out_weights.shape, BF16),
            pltpu.SemaphoreType.DMA((7,)),
            pltpu.SemaphoreType.DMA((4,)),
            pltpu.SemaphoreType.DMA((LAYERS, 4 * planes)),
            pltpu.SemaphoreType.DMA((LAYERS, n)),
            pltpu.SemaphoreType.DMA((LAYERS, 2)),
            pltpu.SemaphoreType.DMA((LAYERS, 2)),
        ],
        compiler_params=pltpu.CompilerParams(
            collective_id=0, has_side_effects=True, vmem_limit_bytes=48 * 1024 * 1024
        ),
    )(
        reverse_block.reshape(1, EBLK),
        block_atom.reshape(1, EBLK),
        edge_state,
        atom_state,
        target_row.reshape(EBLK, NB),
        reverse_lane.reshape(EBLK, NB),
        source_atom.reshape(EBLK, NB),
        edge_weights,
        atom_in_weights,
        atom_out_weights,
    )
    edges = pl.pallas_call(
        unsort,
        out_shape=jax.ShapeDtypeStruct((e_dev, de), BF16),
        in_specs=[smem, anys],
        out_specs=anys,
        scratch_shapes=[pltpu.SemaphoreType.DMA],
    )(pos, ordered)
    return edges, atoms


def solution(mesh):
    both = P(("groups", "graph"))
    rows = P(("groups", "graph"), None)
    return jax.shard_map(
        functools.partial(local, mesh.shape["graph"]),
        mesh=mesh,
        in_specs=(rows, rows, both, both, both, both, both, P(), P(), P()),
        out_specs=(rows, rows),
        check_vma=False,
    )
```

```python
import functools

import jax
import jax.numpy as jnp
from jax import lax
from jax.experimental import pallas as pl
from jax.experimental.pallas import tpu as pltpu
from jax.sharding import PartitionSpec as P

NB = 32
ATB = 16
LAYERS = 2
EBLK = 32
A_DEV = 128
QUARTER = 8
CH = QUARTER * NB
MESH = pl.DeviceIdType.MESH
F32 = jnp.float32
BF16 = jnp.bfloat16


def dot(a, b):
    return jnp.dot(a, b, preferred_element_type=F32)


def silu(v):
    return (0.5 * v) * (1.0 + jnp.tanh(0.5 * v))


def hot(mask):
    return jnp.where(mask, 1.0, 0.0).astype(BF16)


def kernel(
    n,
    rblock_hbm,
    batom_hbm,
    edge_hbm,
    atom_hbm,
    trow_hbm,
    rlane_hbm,
    satom_hbm,
    ew_hbm,
    aw_hbm,
    ow_hbm,
    edges,
    atom_out,
    pos_out,
    rblock,
    batom,
    atom_in,
    trow,
    rlane,
    satom,
    raw,
    ohe,
    upd,
    part,
    oht,
    ohs,
    ohr,
    ohc,
    table,
    recv_up,
    recv_dn,
    ew,
    aw,
    ow,
    load_sem,
    ag_send,
    ag_recv,
    x_send,
    x_recv,
):
    me = lax.axis_index("graph")
    planes = n // 4
    y = (me // 2) % 2
    c = me % 2
    y_peer = me + 2 - 4 * y
    s_peer = me + 1 - 2 * c
    s_y_peer = s_peer + 2 - 4 * y
    has_up = me < n - 1
    has_dn = me > 0

    order = [
        (atom_hbm, atom_in),
        (rblock_hbm, rblock),
        (batom_hbm, batom),
        (trow_hbm, trow),
        (rlane_hbm, rlane),
        (satom_hbm, satom),
        (edge_hbm, raw),
    ]
    for l in range(LAYERS):
        order += [(aw_hbm.at[l], aw.at[l]), (ew_hbm.at[l], ew.at[l]), (ow_hbm.at[l], ow.at[l])]
    loads = []
    for i, (src, dst) in enumerate(order):
        loads.append(pltpu.make_async_copy(src, dst, load_sem.at[i]))
    for cp in loads:
        cp.start()

    barrier = pltpu.get_barrier_semaphore()

    def greet(dev):
        pl.semaphore_signal(barrier, inc=1, device_id={"graph": dev}, device_id_type=MESH)

    for d in range(1, planes):
        greet((me + 4 * d) % n)
    greet(y_peer)
    greet(s_peer)

    greet((me + n + 2 * c - 1) % n)
    pl.semaphore_wait(barrier, planes + 2)

    def shard_rows(dev):
        return pl.ds(pl.multiple_of(dev * A_DEV, A_DEV), A_DEV)

    sent = []

    def push(l, shard, dev):
        rows = shard_rows(shard)
        cp = pltpu.make_async_remote_copy(
            src_ref=table.at[l, rows],
            dst_ref=table.at[l, rows],
            send_sem=ag_send.at[l, len(sent) % (4 * planes)],
            recv_sem=ag_recv.at[l, shard],
            device_id={"graph": dev},
            device_id_type=MESH,
        )
        cp.start()
        sent.append(cp)

    def arrived(l, shard):
        rows = shard_rows(shard)
        pltpu.make_async_remote_copy(
            src_ref=table.at[l, rows],
            dst_ref=table.at[l, rows],
            send_sem=ag_send.at[l, 0],
            recv_sem=ag_recv.at[l, shard],
            device_id={"graph": s_peer},
            device_id_type=MESH,
        ).wait_recv()

    def exchange(l, up):
        return pltpu.make_async_remote_copy(
            src_ref=upd.at[pl.ds(0 if up else CH, CH)],
            dst_ref=recv_dn.at[l] if up else recv_up.at[l],
            send_sem=x_send.at[l, 0 if up else 1],
            recv_sem=x_recv.at[l, 0 if up else 1],
            device_id={"graph": me + 1 if up else me - 1},
            device_id_type=MESH,
        )

    def block_order(key, is_up, is_dn, rank):
        n_up = jnp.where(has_up, QUARTER, 0)
        inner = rank - n_up - jnp.where(has_dn, QUARTER, 0)
        first_base = jnp.where(has_dn, jnp.where(has_up, 2 * QUARTER, 0), QUARTER)
        later_base = jnp.where(has_dn, jnp.where(has_up, 2 * QUARTER, QUARTER), QUARTER)
        inner = jnp.where(inner < QUARTER, inner + first_base, inner + later_base)
        return jnp.where(is_up, rank, jnp.where(is_dn, QUARTER + rank - n_up, inner))

    def prepare():
        square = (EBLK, EBLK)
        lanes = lax.broadcasted_iota(jnp.int32, square, 1)
        subs = lax.broadcasted_iota(jnp.int32, square, 0)
        rb = jnp.broadcast_to(rblock[...], square)
        low = me * EBLK
        is_up = rb >= low + EBLK
        is_dn = rb < low
        mine = lanes + low
        inner_key = 2 * jnp.minimum(mine, rb) + jnp.where(mine > rb, 1, 0)
        big = 4 * n * EBLK
        key = jnp.where(is_up, lanes, jnp.where(is_dn, big + rb, 2 * big + inner_key))
        rank = jnp.sum(jnp.where(key.T < key, 1, 0), axis=0, keepdims=True)
        pos = block_order(key, is_up, is_dn, jnp.broadcast_to(rank, square))
        pos_out[...] = pos[0:1, :]
        here = pos == subs
        pcol = jnp.sum(jnp.where(here, lanes, 0), axis=1, keepdims=True)
        bcol = jnp.sum(jnp.where(here, jnp.broadcast_to(batom[...], square), 0), axis=1, keepdims=True)
        per_row = 128 // NB
        pick = hot(pcol == per_row * (lanes % 8) + lanes // 8)

        def by_slot(ref):
            flat = ref[...].astype(F32)
            blocks = jnp.concatenate([flat[:, j * NB : (j + 1) * NB] for j in range(per_row)], axis=0)
            return dot(pick, blocks.astype(BF16)).T.astype(jnp.int32)

        tcol = by_slot(trow)
        scol = by_slot(satom)
        rcol = by_slot(rlane)
        wide = lax.broadcasted_iota(jnp.int32, (NB, CH), 1)
        narrow = lax.broadcasted_iota(jnp.int32, (NB, A_DEV), 1)
        for p in range(EBLK):
            rows = pl.ds(p * NB, NB)
            oht[rows, :] = hot(wide == tcol[:, p : p + 1] + (p % 16) * ATB)
            ohs[rows, :] = hot(narrow == scol[:, p : p + 1])
            slot = p % QUARTER
            swapped = (slot ^ 1) * NB
            if p < 2 * QUARTER:
                remote = has_up if p < QUARTER else has_dn
                off = jnp.where(remote, slot * NB, swapped)
            else:
                off = swapped
            ohr[rows, :] = hot(wide == rcol[:, p : p + 1] + off)
        e_dev = raw.shape[0]
        from_edge = lax.broadcasted_iota(jnp.int32, (NB, e_dev), 1) - lax.broadcasted_iota(jnp.int32, (NB, e_dev), 0)
        for p in range(EBLK):
            ohe[pl.ds(p * NB, NB), :] = hot(from_edge == pcol[p : p + 1, :] * NB)
        atoms_all = n * A_DEV
        from_atom = lax.broadcasted_iota(jnp.int32, (ATB, atoms_all), 1) - lax.broadcasted_iota(jnp.int32, (ATB, atoms_all), 0)
        for p in range(EBLK):
            ohc[pl.ds(p * ATB, ATB), :] = hot(from_atom == bcol[p : p + 1, :] * ATB)

    def sort_edges():
        loads[6].wait()
        for q in range(4):
            rows = pl.ds(q * CH, CH)
            edges[rows, :] = dot(ohe[rows, :], raw[...]).astype(BF16)

    for l in range(LAYERS):
        atoms = atom_in if l == 0 else atom_out
        del sent[:]
        if l == 0:
            loads[0].wait()
        table[l, shard_rows(me), :] = atoms[...]
        push(l, me, y_peer)
        for d in range(1, planes):
            push(l, me, (me + 4 * d) % n)
        push(l, me, s_peer)

        if l == 0:
            for cp in loads[1:6]:
                cp.wait()
            prepare()
        for d in range(1, planes):
            shard = (me + n - 4 * d) % n
            arrived(l, shard)
            push(l, shard, y_peer)
            push(l, shard, s_peer)
        if l == 0:
            sort_edges()
            loads[7].wait()
            loads[8].wait()
        for d in range(planes):
            shard = (y_peer + n - 4 * d) % n
            arrived(l, shard)
            push(l, shard, s_peer)

        sproj = dot(atoms[...], aw[l, 1]).astype(BF16)
        for q in range(4):
            rows = pl.ds(q * CH, CH)
            part[rows, :] = dot(edges[rows, :], ew[l, 0]) + dot(ohs[rows, :], sproj)

        for d in range(planes):
            arrived(l, (s_peer + n - 4 * d) % n)
            arrived(l, (s_y_peer + n - 4 * d) % n)

        def project(half):
            chosen = dot(ohc[pl.ds(half * CH, CH), :], table[l]).astype(BF16)
            return dot(chosen, aw[l, 0]).astype(BF16)

        def first(q):
            rows = pl.ds(q * CH, CH)
            h = silu(part[rows, :] + dot(oht[rows, :], tproj)).astype(BF16)
            upd[rows, :] = (edges[rows, :].astype(F32) + dot(h, ew[l, 1])).astype(BF16)

        tproj = project(0)
        first(0)

        @pl.when(has_up)
        def _():
            exchange(l, True).start()

        first(1)

        @pl.when(has_dn)
        def _():
            exchange(l, False).start()

        tproj = project(1)
        first(2)
        first(3)

        if l == 0:
            loads[9].wait()

        def second(q, partner):
            rows = pl.ds(q * CH, CH)
            u = upd[rows, :].astype(F32)
            paired = (u + dot(ohr[rows, :], partner)).astype(BF16)
            g = silu(dot(paired, ew[l, 2])).astype(BF16)
            e = (u + dot(g, ew[l, 3])).astype(BF16)
            edges[rows, :] = e
            return lax.dot_general(ohs[rows, :], e, (((0,), (0,)), ((), ())), preferred_element_type=F32)

        summed = second(2, upd[pl.ds(2 * CH, CH), :])
        summed = summed + second(3, upd[pl.ds(3 * CH, CH), :])

        @pl.when(has_up)
        def _():
            exchange(l, False).wait_recv()

        @pl.when(jnp.logical_not(has_up))
        def _():
            recv_up[l] = upd[pl.ds(0, CH), :]

        summed = summed + second(0, recv_up[l])

        @pl.when(has_dn)
        def _():
            exchange(l, True).wait_recv()

        @pl.when(jnp.logical_not(has_dn))
        def _():
            recv_dn[l] = upd[pl.ds(CH, CH), :]

        summed = summed + second(1, recv_dn[l])

        pooled = (0.35 * summed).astype(BF16)
        atom_out[...] = (atoms[...].astype(F32) + silu(dot(pooled, ow[l]))).astype(BF16)

        for cp in sent:
            cp.wait_send()

        @pl.when(has_up)
        def _():
            exchange(l, True).wait_send()

        @pl.when(has_dn)
        def _():
            exchange(l, False).wait_send()

        if l == 0:
            for cp in loads[10:]:
                cp.wait()


def unsort(pos_in, src, atoms, dst, atoms_dst, pos, sem, atom_sem):
    keep = pltpu.make_async_copy(atoms, atoms_dst, atom_sem)
    keep.start()
    pltpu.sync_copy(pos_in, pos)
    for b in range(EBLK):
        start = pl.multiple_of(pos[0, b] * NB, NB)
        pltpu.make_async_copy(src.at[pl.ds(start, NB)], dst.at[pl.ds(b * NB, NB)], sem).start()
    pltpu.make_async_copy(src, dst, sem).wait()
    keep.wait()


def local(
    n,
    edge_state,
    atom_state,
    block_atom,
    target_row,
    reverse_block,
    reverse_lane,
    source_atom,
    edge_weights,
    atom_in_weights,
    atom_out_weights,
):
    de = edge_state.shape[1]
    da = atom_state.shape[1]
    e_dev = edge_state.shape[0]
    vmem = pl.BlockSpec(memory_space=pltpu.VMEM)
    hbm = pl.BlockSpec(memory_space=pltpu.HBM)
    planes = n // 4
    ordered, atoms, pos = pl.pallas_call(
        functools.partial(kernel, n),
        out_shape=(
            jax.ShapeDtypeStruct((e_dev, de), BF16),
            jax.ShapeDtypeStruct((A_DEV, da), BF16),
            jax.ShapeDtypeStruct((1, EBLK), jnp.int32),
        ),
        in_specs=[hbm] * 10,
        out_specs=(vmem, vmem, vmem),
        scratch_shapes=[
            pltpu.VMEM((1, EBLK), jnp.int32),
            pltpu.VMEM((1, EBLK), jnp.int32),
            pltpu.VMEM((A_DEV, da), BF16),
            pltpu.VMEM((8, e_dev // 8), jnp.int32),
            pltpu.VMEM((8, e_dev // 8), jnp.int32),
            pltpu.VMEM((8, e_dev // 8), jnp.int32),
            pltpu.VMEM((e_dev, de), BF16),
            pltpu.VMEM((e_dev, e_dev), BF16),
            pltpu.VMEM((e_dev, de), BF16),
            pltpu.VMEM((e_dev, de), F32),
            pltpu.VMEM((e_dev, CH), BF16),
            pltpu.VMEM((e_dev, A_DEV), BF16),
            pltpu.VMEM((e_dev, CH), BF16),
            pltpu.VMEM((EBLK * ATB, n * A_DEV), BF16),
            pltpu.VMEM((LAYERS, n * A_DEV, da), BF16),
            pltpu.VMEM((LAYERS, CH, de), BF16),
            pltpu.VMEM((LAYERS, CH, de), BF16),
            pltpu.VMEM(edge_weights.shape, BF16),
            pltpu.VMEM(atom_in_weights.shape, BF16),
            pltpu.VMEM(atom_out_weights.shape, BF16),
            pltpu.SemaphoreType.DMA((13,)),
            pltpu.SemaphoreType.DMA((LAYERS, 4 * planes)),
            pltpu.SemaphoreType.DMA((LAYERS, n)),
            pltpu.SemaphoreType.DMA((LAYERS, 2)),
            pltpu.SemaphoreType.DMA((LAYERS, 2)),
        ],
        compiler_params=pltpu.CompilerParams(
            collective_id=0, has_side_effects=True, vmem_limit_bytes=62 * 1024 * 1024
        ),
    )(
        reverse_block.reshape(1, EBLK),
        block_atom.reshape(1, EBLK),
        edge_state,
        atom_state,
        target_row.reshape(8, e_dev // 8),
        reverse_lane.reshape(8, e_dev // 8),
        source_atom.reshape(8, e_dev // 8),
        edge_weights,
        atom_in_weights,
        atom_out_weights,
    )
    return pl.pallas_call(
        unsort,
        out_shape=(
            jax.ShapeDtypeStruct((e_dev, de), BF16),
            jax.ShapeDtypeStruct((A_DEV, da), BF16),
        ),
        in_specs=[vmem, vmem, vmem],
        out_specs=(hbm, hbm),
        scratch_shapes=[pltpu.SMEM((1, EBLK), jnp.int32), pltpu.SemaphoreType.DMA, pltpu.SemaphoreType.DMA],
    )(pos, ordered, atoms)


def solution(mesh):
    both = P(("groups", "graph"))
    rows = P(("groups", "graph"), None)
    return jax.shard_map(
        functools.partial(local, mesh.shape["graph"]),
        mesh=mesh,
        in_specs=(rows, rows, both, both, both, both, both, P(), P(), P()),
        out_specs=(rows, rows),
        check_vma=False,
    )
```

```python
import functools

import jax
import jax.numpy as jnp
from jax import lax
from jax.experimental import pallas as pl
from jax.experimental.pallas import tpu as pltpu
from jax.sharding import PartitionSpec as P

NB = 32
ATB = 16
LAYERS = 2
EBLK = 32
A_DEV = 128
QUARTER = 8
CH = QUARTER * NB
MESH = pl.DeviceIdType.MESH
F32 = jnp.float32
BF16 = jnp.bfloat16


def dot(a, b):
    return jnp.dot(a, b, preferred_element_type=F32)


def silu(v):
    return (0.5 * v) * (1.0 + jnp.tanh(0.5 * v))


def hot(mask):
    return jnp.where(mask, 1.0, 0.0).astype(BF16)


def kernel(
    n,
    rblock_hbm,
    batom_hbm,
    edge_hbm,
    atom_hbm,
    trow_hbm,
    rlane_hbm,
    satom_hbm,
    ew_hbm,
    aw_hbm,
    ow_hbm,
    edges,
    atom_out,
    pos_out,
    rblock,
    batom,
    atom_in,
    trow,
    rlane,
    satom,
    raw,
    ohe,
    upd,
    part,
    oht,
    ohs,
    ohr,
    ohc,
    table,
    recv_up,
    recv_dn,
    ew,
    aw,
    ow,
    load_sem,
    ag_send,
    ag_recv,
    x_send,
    x_recv,
):
    me = lax.axis_index("graph")
    planes = n // 4
    y = (me // 2) % 2
    c = me % 2
    y_peer = me + 2 - 4 * y
    s_peer = me + 1 - 2 * c
    s_y_peer = s_peer + 2 - 4 * y
    has_up = me < n - 1
    has_dn = me > 0

    order = [
        (atom_hbm, atom_in),
        (rblock_hbm, rblock),
        (batom_hbm, batom),
        (trow_hbm, trow),
        (rlane_hbm, rlane),
        (satom_hbm, satom),
        (edge_hbm, raw),
    ]
    for l in range(LAYERS):
        order += [(aw_hbm.at[l], aw.at[l]), (ew_hbm.at[l], ew.at[l]), (ow_hbm.at[l], ow.at[l])]
    loads = []
    for i, (src, dst) in enumerate(order):
        loads.append(pltpu.make_async_copy(src, dst, load_sem.at[i]))
    for cp in loads:
        cp.start()

    barrier = pltpu.get_barrier_semaphore()

    def greet(dev):
        pl.semaphore_signal(barrier, inc=1, device_id={"graph": dev}, device_id_type=MESH)

    for d in range(1, planes):
        greet((me + 4 * d) % n)
    greet(y_peer)
    greet(s_peer)

    greet((me + n + 2 * c - 1) % n)
    pl.semaphore_wait(barrier, planes + 2)

    def shard_rows(dev):
        return pl.ds(pl.multiple_of(dev * A_DEV, A_DEV), A_DEV)

    sent = []

    def push(l, shard, dev):
        rows = shard_rows(shard)
        cp = pltpu.make_async_remote_copy(
            src_ref=table.at[l, rows],
            dst_ref=table.at[l, rows],
            send_sem=ag_send.at[l, len(sent) % (4 * planes)],
            recv_sem=ag_recv.at[l, shard],
            device_id={"graph": dev},
            device_id_type=MESH,
        )
        cp.start()
        sent.append(cp)

    def arrived(l, shard):
        rows = shard_rows(shard)
        pltpu.make_async_remote_copy(
            src_ref=table.at[l, rows],
            dst_ref=table.at[l, rows],
            send_sem=ag_send.at[l, 0],
            recv_sem=ag_recv.at[l, shard],
            device_id={"graph": s_peer},
            device_id_type=MESH,
        ).wait_recv()

    def exchange(l, up):
        return pltpu.make_async_remote_copy(
            src_ref=upd.at[pl.ds(0 if up else CH, CH)],
            dst_ref=recv_dn.at[l] if up else recv_up.at[l],
            send_sem=x_send.at[l, 0 if up else 1],
            recv_sem=x_recv.at[l, 0 if up else 1],
            device_id={"graph": me + 1 if up else me - 1},
            device_id_type=MESH,
        )

    def block_order(key, is_up, is_dn, rank):
        n_up = jnp.where(has_up, QUARTER, 0)
        inner = rank - n_up - jnp.where(has_dn, QUARTER, 0)
        first_base = jnp.where(has_dn, jnp.where(has_up, 2 * QUARTER, 0), QUARTER)
        later_base = jnp.where(has_dn, jnp.where(has_up, 2 * QUARTER, QUARTER), QUARTER)
        inner = jnp.where(inner < QUARTER, inner + first_base, inner + later_base)
        return jnp.where(is_up, rank, jnp.where(is_dn, QUARTER + rank - n_up, inner))

    def prepare():
        square = (EBLK, EBLK)
        lanes = lax.broadcasted_iota(jnp.int32, square, 1)
        subs = lax.broadcasted_iota(jnp.int32, square, 0)
        rb = jnp.broadcast_to(rblock[...], square)
        low = me * EBLK
        is_up = rb >= low + EBLK
        is_dn = rb < low
        mine = lanes + low
        inner_key = 2 * jnp.minimum(mine, rb) + jnp.where(mine > rb, 1, 0)
        big = 4 * n * EBLK
        key = jnp.where(is_up, lanes, jnp.where(is_dn, big + rb, 2 * big + inner_key))
        rank = jnp.sum(jnp.where(key.T < key, 1, 0), axis=0, keepdims=True)
        pos = block_order(key, is_up, is_dn, jnp.broadcast_to(rank, square))
        pos_out[...] = pos[0:1, :]
        here = pos == subs
        pcol = jnp.sum(jnp.where(here, lanes, 0), axis=1, keepdims=True)
        bcol = jnp.sum(jnp.where(here, jnp.broadcast_to(batom[...], square), 0), axis=1, keepdims=True)
        per_row = 128 // NB
        pick = hot(pcol == per_row * (lanes % 8) + lanes // 8)

        def by_slot(ref):
            flat = ref[...].astype(F32)
            blocks = jnp.concatenate([flat[:, j * NB : (j + 1) * NB] for j in range(per_row)], axis=0)
            return dot(pick, blocks.astype(BF16)).T.astype(jnp.int32)

        tcol = by_slot(trow)
        scol = by_slot(satom)
        rcol = by_slot(rlane)
        wide = lax.broadcasted_iota(jnp.int32, (NB, CH), 1)
        narrow = lax.broadcasted_iota(jnp.int32, (NB, A_DEV), 1)
        for p in range(EBLK):
            rows = pl.ds(p * NB, NB)
            oht[rows, :] = hot(wide == tcol[:, p : p + 1] + (p % 16) * ATB)
            ohs[rows, :] = hot(narrow == scol[:, p : p + 1])
            slot = p % QUARTER
            swapped = (slot ^ 1) * NB
            if p < 2 * QUARTER:
                remote = has_up if p < QUARTER else has_dn
                off = jnp.where(remote, slot * NB, swapped)
            else:
                off = swapped
            ohr[rows, :] = hot(wide == rcol[:, p : p + 1] + off)
        e_dev = raw.shape[0]
        from_edge = lax.broadcasted_iota(jnp.int32, (NB, e_dev), 1) - lax.broadcasted_iota(jnp.int32, (NB, e_dev), 0)
        for p in range(EBLK):
            ohe[pl.ds(p * NB, NB), :] = hot(from_edge == pcol[p : p + 1, :] * NB)
        atoms_all = n * A_DEV
        from_atom = lax.broadcasted_iota(jnp.int32, (ATB, atoms_all), 1) - lax.broadcasted_iota(jnp.int32, (ATB, atoms_all), 0)
        for p in range(EBLK):
            ohc[pl.ds(p * ATB, ATB), :] = hot(from_atom == bcol[p : p + 1, :] * ATB)

    def sort_edges():
        loads[6].wait()
        for q in range(4):
            rows = pl.ds(q * CH, CH)
            edges[rows, :] = dot(ohe[rows, :], raw[...]).astype(BF16)

    for l in range(LAYERS):
        atoms = atom_in if l == 0 else atom_out
        del sent[:]
        if l == 0:
            loads[0].wait()
        table[l, shard_rows(me), :] = atoms[...]
        push(l, me, y_peer)
        for d in range(1, planes):
            push(l, me, (me + 4 * d) % n)
        push(l, me, s_peer)

        def own_part():
            sproj = dot(atoms[...], aw[l, 1]).astype(BF16)
            for q in range(4):
                rows = pl.ds(q * CH, CH)
                part[rows, :] = dot(edges[rows, :], ew[l, 0]) + dot(ohs[rows, :], sproj)

        if l == 0:
            for cp in loads[1:6]:
                cp.wait()
            prepare()
        else:
            own_part()
        for d in range(1, planes):
            shard = (me + n - 4 * d) % n
            arrived(l, shard)
            push(l, shard, y_peer)
            push(l, shard, s_peer)
        if l == 0:
            sort_edges()
            loads[7].wait()
            loads[8].wait()
        for d in range(planes):
            shard = (y_peer + n - 4 * d) % n
            arrived(l, shard)
            push(l, shard, s_peer)

        if l == 0:
            own_part()

        for d in range(planes):
            arrived(l, (s_peer + n - 4 * d) % n)
            arrived(l, (s_y_peer + n - 4 * d) % n)

        def project(half):
            chosen = dot(ohc[pl.ds(half * CH, CH), :], table[l]).astype(BF16)
            return dot(chosen, aw[l, 0]).astype(BF16)

        def first(q):
            rows = pl.ds(q * CH, CH)
            h = silu(part[rows, :] + dot(oht[rows, :], tproj)).astype(BF16)
            upd[rows, :] = (edges[rows, :].astype(F32) + dot(h, ew[l, 1])).astype(BF16)

        tproj = project(0)
        first(0)

        @pl.when(has_up)
        def _():
            exchange(l, True).start()

        first(1)

        @pl.when(has_dn)
        def _():
            exchange(l, False).start()

        tproj = project(1)
        first(2)
        first(3)

        if l == 0:
            loads[9].wait()

        def second(q, partner):
            rows = pl.ds(q * CH, CH)
            u = upd[rows, :].astype(F32)
            paired = (u + dot(ohr[rows, :], partner)).astype(BF16)
            g = silu(dot(paired, ew[l, 2])).astype(BF16)
            e = (u + dot(g, ew[l, 3])).astype(BF16)
            edges[rows, :] = e
            return lax.dot_general(ohs[rows, :], e, (((0,), (0,)), ((), ())), preferred_element_type=F32)

        summed = second(2, upd[pl.ds(2 * CH, CH), :])
        summed = summed + second(3, upd[pl.ds(3 * CH, CH), :])

        @pl.when(has_up)
        def _():
            exchange(l, False).wait_recv()

        @pl.when(jnp.logical_not(has_up))
        def _():
            recv_up[l] = upd[pl.ds(0, CH), :]

        summed = summed + second(0, recv_up[l])

        @pl.when(has_dn)
        def _():
            exchange(l, True).wait_recv()

        @pl.when(jnp.logical_not(has_dn))
        def _():
            recv_dn[l] = upd[pl.ds(CH, CH), :]

        summed = summed + second(1, recv_dn[l])

        pooled = (0.35 * summed).astype(BF16)
        atom_out[...] = (atoms[...].astype(F32) + silu(dot(pooled, ow[l]))).astype(BF16)

        for cp in sent:
            cp.wait_send()

        @pl.when(has_up)
        def _():
            exchange(l, True).wait_send()

        @pl.when(has_dn)
        def _():
            exchange(l, False).wait_send()

        if l == 0:
            for cp in loads[10:]:
                cp.wait()


def unsort(pos_in, src, atoms, dst, atoms_dst, pos, sem, atom_sem):
    keep = pltpu.make_async_copy(atoms, atoms_dst, atom_sem)
    keep.start()
    pltpu.sync_copy(pos_in, pos)
    for b in range(EBLK):
        start = pl.multiple_of(pos[0, b] * NB, NB)
        pltpu.make_async_copy(src.at[pl.ds(start, NB)], dst.at[pl.ds(b * NB, NB)], sem).start()
    pltpu.make_async_copy(src, dst, sem).wait()
    keep.wait()


def local(
    n,
    edge_state,
    atom_state,
    block_atom,
    target_row,
    reverse_block,
    reverse_lane,
    source_atom,
    edge_weights,
    atom_in_weights,
    atom_out_weights,
):
    de = edge_state.shape[1]
    da = atom_state.shape[1]
    e_dev = edge_state.shape[0]
    vmem = pl.BlockSpec(memory_space=pltpu.VMEM)
    hbm = pl.BlockSpec(memory_space=pltpu.HBM)
    planes = n // 4
    ordered, atoms, pos = pl.pallas_call(
        functools.partial(kernel, n),
        out_shape=(
            jax.ShapeDtypeStruct((e_dev, de), BF16),
            jax.ShapeDtypeStruct((A_DEV, da), BF16),
            jax.ShapeDtypeStruct((1, EBLK), jnp.int32),
        ),
        in_specs=[hbm] * 10,
        out_specs=(vmem, vmem, vmem),
        scratch_shapes=[
            pltpu.VMEM((1, EBLK), jnp.int32),
            pltpu.VMEM((1, EBLK), jnp.int32),
            pltpu.VMEM((A_DEV, da), BF16),
            pltpu.VMEM((8, e_dev // 8), jnp.int32),
            pltpu.VMEM((8, e_dev // 8), jnp.int32),
            pltpu.VMEM((8, e_dev // 8), jnp.int32),
            pltpu.VMEM((e_dev, de), BF16),
            pltpu.VMEM((e_dev, e_dev), BF16),
            pltpu.VMEM((e_dev, de), BF16),
            pltpu.VMEM((e_dev, de), F32),
            pltpu.VMEM((e_dev, CH), BF16),
            pltpu.VMEM((e_dev, A_DEV), BF16),
            pltpu.VMEM((e_dev, CH), BF16),
            pltpu.VMEM((EBLK * ATB, n * A_DEV), BF16),
            pltpu.VMEM((LAYERS, n * A_DEV, da), BF16),
            pltpu.VMEM((LAYERS, CH, de), BF16),
            pltpu.VMEM((LAYERS, CH, de), BF16),
            pltpu.VMEM(edge_weights.shape, BF16),
            pltpu.VMEM(atom_in_weights.shape, BF16),
            pltpu.VMEM(atom_out_weights.shape, BF16),
            pltpu.SemaphoreType.DMA((13,)),
            pltpu.SemaphoreType.DMA((LAYERS, 4 * planes)),
            pltpu.SemaphoreType.DMA((LAYERS, n)),
            pltpu.SemaphoreType.DMA((LAYERS, 2)),
            pltpu.SemaphoreType.DMA((LAYERS, 2)),
        ],
        compiler_params=pltpu.CompilerParams(
            collective_id=0, has_side_effects=True, vmem_limit_bytes=62 * 1024 * 1024
        ),
    )(
        reverse_block.reshape(1, EBLK),
        block_atom.reshape(1, EBLK),
        edge_state,
        atom_state,
        target_row.reshape(8, e_dev // 8),
        reverse_lane.reshape(8, e_dev // 8),
        source_atom.reshape(8, e_dev // 8),
        edge_weights,
        atom_in_weights,
        atom_out_weights,
    )
    return pl.pallas_call(
        unsort,
        out_shape=(
            jax.ShapeDtypeStruct((e_dev, de), BF16),
            jax.ShapeDtypeStruct((A_DEV, da), BF16),
        ),
        in_specs=[vmem, vmem, vmem],
        out_specs=(hbm, hbm),
        scratch_shapes=[pltpu.SMEM((1, EBLK), jnp.int32), pltpu.SemaphoreType.DMA, pltpu.SemaphoreType.DMA],
    )(pos, ordered, atoms)


def solution(mesh):
    both = P(("groups", "graph"))
    rows = P(("groups", "graph"), None)
    return jax.shard_map(
        functools.partial(local, mesh.shape["graph"]),
        mesh=mesh,
        in_specs=(rows, rows, both, both, both, both, both, P(), P(), P()),
        out_specs=(rows, rows),
        check_vma=False,
    )
```
